32 devices in a mesh: parts: 2 (over y), expert: 4 (over z), tensor: 2 (over x), seq: 2 (over core).
Axes of the slice: x: 2, y: 2, z: 4, core: 2. Of those that a mesh axis runs over, the one named last changes fastest.
Arguments:
- tokens: bfloat16 [128, 4096], P(('parts', 'expert', 'tensor', 'seq')), parts along dimension 0, may hold values from -6 to 6
- out_grad: bfloat16 [128, 4096], P(('parts', 'expert', 'tensor', 'seq')), parts along dimension 0, may hold values from -3 to 3
- expert_ids: int32 [128, 2], P(('parts', 'expert', 'tensor', 'seq')), parts along dimension 0, may hold values from 0 to 3, all different within a row; in each aligned block of 4 rows (0 to 3, 4 to 7, ...) at most 3 rows name the same one
- probs: bfloat16 [128, 2], P(('parts', 'expert', 'tensor', 'seq')), parts along dimension 0, may hold values from 0.19921875 to 1
- w_gate: bfloat16 [4, 4096, 8192], P('expert', None, ('tensor', 'seq')), may hold values from -0.09375 to 0.09375
- w_up: bfloat16 [4, 4096, 8192], P('expert', None, ('tensor', 'seq')), may hold values from -0.09375 to 0.09375
- w_down: bfloat16 [4, 8192, 4096], P('expert', ('tensor', 'seq')), may hold values from -0.0625 to 0.0625
Outputs:
- grad_tokens: float32 [128, 4096], P(('parts', 'expert', 'tensor', 'seq')), parts along dimension 0
- grad_probs: float32 [128, 2], P(('parts', 'expert', 'tensor', 'seq')), parts along dimension 0
- grad_gate: bfloat16 [8, 4096, 8192], P(('parts', 'expert'), None, ('tensor', 'seq')), parts along dimension 0
- grad_up: bfloat16 [8, 4096, 8192], P(('parts', 'expert'), None, ('tensor', 'seq')), parts along dimension 0
- grad_down: bfloat16 [8, 8192, 4096], P(('parts', 'expert'), ('tensor', 'seq')), parts along dimension 0
The draws below stay inside these ranges and needn't reach their ends.
There are 2 independent parts, one for each index of `parts`. The reference program is written for one: setup_inputs(seed, part) draws one part's arguments, and reference() takes and returns one part's arrays. A program takes and returns all parts, laid end to end along the dimension named above; an argument that names none is the same for every part. Nothing has to cross between parts.
Inputs may be any that keep to these rules, and one draw needn't show every extreme that they name: `expert_ids`: each row names 2 different experts. Within the rows of one device (aligned blocks of 4 rows) no expert is named by more than 3 rows, a bound that some block reaches.
All inputs are finite; a program needn't handle non-finite values.
Results may differ from the reference program's by a relative error of at most 0.005.
Values may be sent and summed in bfloat16 or wider, within the bound.
No kernel may reach another device: no remote copies, remote signals or barrier semaphores. Data moves between devices by JAX's collectives and lax.ppermute only.
A program may use at most 192 MiB of HBM per device.

```python
import math
import jax
import jax.numpy as jnp
import numpy as np
from jax import lax

D = 4096
FFW = 8192
EXPERTS = 4
TOP = 2
TOK_DEV = 4
CAP = 3
SPLIT = 1
TOKENS = 64
N_EXPERT = 4


def shard_levels(rng, dims, cuts, least, largest):
    level = 1.0
    for dim, blocks in cuts:
        steps = jax.random.uniform(jax.random.fold_in(jax.random.fold_in(rng, 6), dim), (blocks,), jnp.float32, least / len(cuts), largest / len(cuts))
        level = level * jnp.repeat(jnp.exp(steps), dims[dim] // blocks).reshape((-1,) + (1,) * (len(dims) - 1 - dim))
    return level


def deal_out(stream_key, own, number, rows, number_of, top, reach, skew):
    sequence = jax.random.permutation(stream_key, number_of)
    packed, ordinary = portions_of(number_of, rows * top, reach, skew, True), portions_of(number_of, rows * top, reach, skew, False)
    places = jnp.arange(number_of)

    def named(tallies, offset_by):
        used = int((tallies > 0).sum())
        fixed = max(1, used // 4)
        moved = fixed + (places - fixed + offset_by * (used - fixed)) % max(1, number_of - fixed)
        return jnp.zeros((number_of,), jnp.int32).at[sequence[jnp.where(places < fixed, places, moved)]].set(jnp.asarray(tallies, jnp.int32))

    tallies = jnp.where(number % 4 == 0, named(packed, number // 4), named(ordinary, number - number // 4 - 1))
    mixed = jax.random.permutation(jax.random.fold_in(own, 3), number_of)
    source_of, sink = mixed[0:number_of // 2 * 2:2], mixed[1:number_of // 2 * 2:2]
    margin = jnp.minimum(tallies[source_of] - 1, reach - tallies[sink]) // 2
    margin = jnp.where((source_of == sequence[0]) | (sink == sequence[0]) | (tallies[sink] == 0), 0, jnp.maximum(margin, 0))
    moved = jax.random.randint(jax.random.fold_in(own, 4), (number_of // 2,), 0, 1 << 20) % (margin + 1)
    tallies = tallies.at[source_of].add(-moved).at[sink].add(moved)
    items = jnp.searchsorted(jnp.cumsum(tallies), jnp.arange(rows * top), side="right").astype(jnp.int32)
    table = items.reshape(top, rows).T
    table = table[jax.random.permutation(jax.random.fold_in(own, 1), rows)]
    offset_by = jax.random.randint(jax.random.fold_in(own, 2), (rows, 1), 0, top)
    return jnp.take_along_axis(table, (jnp.arange(top)[None, :] + offset_by) % top, axis=1)


def portions_of(count, total, limit, lean, full):
    portions = [(1 << 20) // math.isqrt(standing ** lean) + 1 for standing in range(1, count + 1)]
    largest = limit if full else min(limit, max(-(-total // count), total * portions[0] // sum(portions)))
    least = 1 if total - largest >= count - 1 else 0
    counts, rest = [largest] + [least] * (count - 1), total - largest - least * (count - 1)
    while rest > 0:
        movable = [i for i in range(1, count) if counts[i] < largest] or [i for i in range(1, count) if counts[i] < limit]
        pool, budget = sum([portions[i] for i in movable]), rest
        for i in movable:
            more = min(limit - counts[i], max(1, budget * portions[i] // pool), rest)
            counts[i] = counts[i] + more
            rest = rest - more
    return np.array(counts)


def centred(key, dims, deviation, bound, cuts=(), kind=jnp.bfloat16):
    gain = shard_levels(key, dims, cuts, -0.22, 0.18) if cuts else 1.0
    drawn = jax.random.normal(key, dims, jnp.float32) * deviation * gain
    return jnp.minimum(jnp.maximum(drawn, -bound), bound).astype(kind)


def setup_inputs(seed: int = 0, part: int = 0) -> dict:
    key_of = jax.random.split(jax.random.key(seed), 8)
    part_splits = jax.random.split(jax.random.fold_in(key_of[7], part), 8)
    tokens = centred(part_splits[0], (TOKENS, D), 1.0, 6.0, ((0, 16),))
    out_grad = centred(part_splits[1], (TOKENS, D), 0.5, 3.0, ((0, 16),))
    expert_ids_keys = jax.random.split(jax.random.fold_in(part_splits[2], 1), TOKENS // TOK_DEV)
    expert_ids_turns = jax.random.permutation(jax.random.fold_in(part_splits[2], 3), TOKENS // TOK_DEV)
    expert_ids = jax.vmap(lambda own, number: deal_out(jax.random.fold_in(part_splits[2], 2), own, number, TOK_DEV, EXPERTS, TOP, CAP, 2))(expert_ids_keys, expert_ids_turns).reshape((TOKENS, TOP))
    probs = jnp.clip(0.19921875 + 0.80078125 * jax.random.uniform(part_splits[3], (TOKENS, TOP), jnp.float32) ** shard_levels(part_splits[3], (TOKENS, TOP), ((0, 16),), -0.2, 0.2), 0.19921875, 1.0).astype(jnp.bfloat16)
    w_gate = centred(key_of[4], (N_EXPERT, D, FFW // SPLIT), D ** -0.5, 0.09375, ((0, 4), (2, 4)))
    w_up = centred(key_of[5], (N_EXPERT, D, FFW // SPLIT), D ** -0.5, 0.09375, ((0, 4), (2, 4)))
    w_down = centred(key_of[6], (N_EXPERT, FFW // SPLIT, D), FFW ** -0.5, 0.0625, ((0, 4), (1, 4)))
    return {"tokens": tokens, "out_grad": out_grad, "expert_ids": expert_ids, "probs": probs, "w_gate": w_gate, "w_up": w_up, "w_down": w_down}


def silu_parts(gate):
    sigma = jax.nn.sigmoid(gate)
    return gate * sigma, sigma * (1.0 + gate * (1.0 - sigma))


def reference(tokens, out_grad, expert_ids, probs, w_gate, w_up, w_down):
    total = tokens.shape[0]
    sources = total // TOK_DEV
    split = N_EXPERT // EXPERTS
    local = FFW // split
    ids = expert_ids.reshape(sources, TOK_DEV * TOP)
    onehot = (ids[:, :, None] == jnp.arange(EXPERTS, dtype=jnp.int32)[None, None, :]).astype(jnp.int32)
    before = jnp.cumsum(onehot, axis=1) - onehot
    slot = jnp.sum(before * onehot, axis=2)
    anchor = jnp.arange(sources, dtype=jnp.int32)[:, None]
    place = ((ids * sources + anchor) * CAP + slot).reshape(-1).astype(jnp.int32)
    rows_total = EXPERTS * sources * CAP
    owner_token = (jnp.arange(total * TOP, dtype=jnp.int32) // TOP).astype(jnp.int32)
    table = jnp.full((rows_total,), total, jnp.int32).at[place].set(owner_token)
    scales = jnp.zeros((rows_total,), jnp.float32).at[place].set(probs.reshape(-1).astype(jnp.float32))
    padded_x = jnp.concatenate([tokens, jnp.zeros((1, D), tokens.dtype)], axis=0)
    padded_dy = jnp.concatenate([out_grad, jnp.zeros((1, D), out_grad.dtype)], axis=0)
    gate_full = w_gate.reshape(EXPERTS, split, D, local).transpose(0, 2, 1, 3).reshape(EXPERTS, D, FFW)
    up_full = w_up.reshape(EXPERTS, split, D, local).transpose(0, 2, 1, 3).reshape(EXPERTS, D, FFW)
    down_full = w_down.reshape(EXPERTS, FFW, D)

    def one_expert(inputs):
        index, scale, w_g, w_u, w_d = inputs
        rows_x = padded_x[index]
        rows_dy = padded_dy[index]
        scale = scale[:, None]
        gate = jnp.dot(rows_x, w_g, preferred_element_type=jnp.float32)
        up = jnp.dot(rows_x, w_u, preferred_element_type=jnp.float32)
        back = lax.dot_general(rows_dy, w_d, (((1,), (1,)), ((), ())), preferred_element_type=jnp.float32)
        act, slope = silu_parts(gate)
        hidden = act * up
        score = jnp.sum(back * hidden, axis=1)
        scaled = scale * back
        d_gate = (scaled * up * slope).astype(jnp.bfloat16)
        d_up = (scaled * act).astype(jnp.bfloat16)
        weighted = (scale * hidden).astype(jnp.bfloat16)
        part_dx = lax.dot_general(d_gate, w_g, (((1,), (1,)), ((), ())), preferred_element_type=jnp.float32)
        part_dx = part_dx + lax.dot_general(d_up, w_u, (((1,), (1,)), ((), ())), preferred_element_type=jnp.float32)
        sum_g = lax.dot_general(rows_x, d_gate, (((0,), (0,)), ((), ())), preferred_element_type=jnp.float32)
        sum_u = lax.dot_general(rows_x, d_up, (((0,), (0,)), ((), ())), preferred_element_type=jnp.float32)
        sum_d = lax.dot_general(weighted, rows_dy, (((0,), (0,)), ((), ())), preferred_element_type=jnp.float32)
        return part_dx, score, sum_g.astype(jnp.bfloat16), sum_u.astype(jnp.bfloat16), sum_d.astype(jnp.bfloat16)

    inputs = (table.reshape(EXPERTS, sources * CAP), scales.reshape(EXPERTS, sources * CAP), gate_full, up_full, down_full)
    part_dx, score, grad_g, grad_u, grad_d = lax.map(one_expert, inputs)
    flat_dx = part_dx.reshape(rows_total, D)
    flat_score = score.reshape(rows_total)
    grad_tokens = jnp.sum(flat_dx[place].reshape(total, TOP, D), axis=1)
    grad_probs = flat_score[place].reshape(total, TOP)
    grad_gate = grad_g.reshape(EXPERTS, D, split, local).transpose(0, 2, 1, 3).reshape(N_EXPERT, D, local)
    grad_up = grad_u.reshape(EXPERTS, D, split, local).transpose(0, 2, 1, 3).reshape(N_EXPERT, D, local)
    grad_down = grad_d.reshape(N_EXPERT, local, D)
    return (grad_tokens, grad_probs, grad_gate, grad_up, grad_down)
```

```python
import functools

import jax
import jax.numpy as jnp
from jax import lax
from jax.experimental import pallas as pl
from jax.experimental.pallas import tpu as pltpu
from jax.sharding import PartitionSpec as P

EXPERTS = 4
TOP = 2
LANES = 128
F32 = jnp.float32
BF16 = jnp.bfloat16
VMEM = pl.BlockSpec(memory_space=pltpu.VMEM)
ANY = pl.BlockSpec(memory_space=pl.ANY)
SMEM = pl.BlockSpec(memory_space=pltpu.SMEM)
MIB = 1 << 20


def tile(size, want):
    while size % want:
        want //= 2
    return want


def rounds(width, hidden):
    return min(width // tile(width, 1024), hidden // tile(hidden, LANES))


def nt(left, right):
    return lax.dot_general(left, right, (((1,), (1,)), ((), ())), preferred_element_type=F32)


def tn(left, right):
    return lax.dot_general(left, right, (((0,), (0,)), ((), ())), preferred_element_type=F32)


def split_sum(value):
    high = value.astype(BF16)
    return high, (value - high.astype(F32)).astype(BF16)


def write_outer(left_ref, right_ref, out_ref, slots, sems, rows, step, steps):
    count = slots.shape[0]
    slot = lax.rem(step, count)
    start = pl.multiple_of(step * rows, rows)

    def copy(index, at):
        return pltpu.make_async_copy(slots.at[index], out_ref.at[0, pl.ds(at, rows)], sems.at[index])

    @pl.when(step >= count)
    def _():
        copy(slot, pl.multiple_of((step - count) * rows, rows)).wait()

    slots[slot] = tn(left_ref[:, pl.ds(start, rows)], right_ref).astype(BF16)
    copy(slot, start).start()


def drain(out_ref, slots, sems, rows, steps):
    count = slots.shape[0]
    for step in range(max(0, steps - count), steps):
        index = step % count
        pltpu.make_async_copy(slots.at[index], out_ref.at[0, pl.ds(step * rows, rows)], sems.at[index]).wait()


def main_kernel(
    width, block, expert_ref, rows_ref, wg_ref, wu_ref, wd_ref,
    keep_ref, send_ref, dg_ref, du_ref, gd_ref, weighted, score, slots, sems,
):
    count = rows_ref.shape[0]
    hidden = wg_ref.shape[2]
    extra = rows_ref[:, 2 * width :].astype(F32)
    lane = lax.broadcasted_iota(jnp.int32, extra.shape, 1)
    mine = jnp.where(lane // TOP == expert_ref[0], extra, 0.0)
    scale = jnp.sum(mine, axis=1, keepdims=True)
    score[...] = jnp.zeros_like(score)
    part = tile(hidden, 1024)

    @pl.loop(0, hidden // part)
    def _(step):
        at = pl.ds(pl.multiple_of(step * part, part), part)
        gate = jnp.dot(rows_ref[:, :width], wg_ref[0, :, at], preferred_element_type=F32)
        up = jnp.dot(rows_ref[:, :width], wu_ref[0, :, at], preferred_element_type=F32)
        back = nt(rows_ref[:, width : 2 * width], wd_ref[0, at, :])
        sigma = jax.nn.sigmoid(gate)
        act = gate * sigma
        slope = sigma * (1.0 + gate * (1.0 - sigma))
        hid = act * up
        score[...] += jnp.sum(back * hid, axis=1, keepdims=True)
        scaled = scale * back
        dg_ref[:, at] = (scaled * up * slope).astype(BF16)
        du_ref[:, at] = (scaled * act).astype(BF16)
        weighted[:, at] = (scale * hid).astype(BF16)

    slot_score = jnp.where(mine > 0.0, score[...], 0.0)
    keep_ref[:, width:] = slot_score[:block]
    high, low = split_sum(slot_score[block:])
    send_ref[:, width : width + LANES] = high
    send_ref[:, width + LANES :] = low

    steps = rounds(width, hidden)
    across = width // steps
    pieces = hidden // steps // slots.shape[1]

    @pl.loop(0, steps)
    def _(step):
        at = pl.ds(pl.multiple_of(step * across, across), across)
        total = nt(dg_ref[...], wg_ref[0, at, :]) + nt(du_ref[...], wu_ref[0, at, :])
        keep_ref[:, at] = total[:block]
        send_ref[:, at] = total[block:].astype(BF16)
        for piece in range(pieces):
            write_outer(
                weighted, rows_ref[:, width : 2 * width], gd_ref, slots, sems, slots.shape[1],
                step * pieces + piece, steps * pieces,
            )

    drain(gd_ref, slots, sems, slots.shape[1], steps * pieces)


def main_call(expert, rows, w_gate, w_up, w_down, block):
    count = rows.shape[0]
    _, width, hidden = w_gate.shape
    w_gate, w_up, w_down = (pltpu.with_memory_space_constraint(w, pltpu.VMEM) for w in (w_gate, w_up, w_down))
    down = tile(hidden // rounds(width, hidden), 256)
    room = 60 * MIB - 3 * 2 * width * hidden
    flops = 2 * count * width * hidden * 6
    return pl.pallas_call(
        functools.partial(main_kernel, width, block),
        out_shape=(
            jax.ShapeDtypeStruct((block, width + LANES), F32),
            jax.ShapeDtypeStruct((count - block, width + 2 * LANES), BF16),
            jax.ShapeDtypeStruct((count, hidden), BF16),
            jax.ShapeDtypeStruct((count, hidden), BF16),
            jax.ShapeDtypeStruct(w_down.shape, BF16),
        ),
        in_specs=[SMEM, VMEM, VMEM, VMEM, VMEM],
        out_specs=(VMEM, VMEM, VMEM, VMEM, ANY),
        scratch_shapes=[
            pltpu.VMEM((count, hidden), BF16),
            pltpu.VMEM((count, 1), F32),
            pltpu.VMEM((2, down, width), BF16),
            pltpu.SemaphoreType.DMA((2,)),
        ],
        compiler_params=pltpu.CompilerParams(vmem_limit_bytes=room),
        cost_estimate=pl.CostEstimate(flops=flops, bytes_accessed=2 * 4 * width * hidden, transcendentals=count * hidden),
        name="hidden_and_inputs",
    )(expert, rows, w_gate, w_up, w_down)


def outer_kernel(width, rows_ref, right_ref, out_ref, slots, sems):
    size = slots.shape[1]
    steps = width // size

    @pl.loop(0, steps)
    def _(step):
        write_outer(rows_ref, right_ref[...], out_ref, slots, sems, size, step, steps)

    drain(out_ref, slots, sems, size, steps)


def outer_call(rows, right, width, name):
    count, hidden = right.shape
    size = tile(width, 512)
    return pl.pallas_call(
        functools.partial(outer_kernel, width),
        out_shape=jax.ShapeDtypeStruct((1, width, hidden), BF16),
        in_specs=[VMEM, VMEM],
        out_specs=ANY,
        scratch_shapes=[pltpu.VMEM((3, size, hidden), BF16), pltpu.SemaphoreType.DMA((3,))],
        compiler_params=pltpu.CompilerParams(vmem_limit_bytes=24 * MIB),
        cost_estimate=pl.CostEstimate(
            flops=2 * count * width * hidden * 4, bytes_accessed=2 * width * hidden, transcendentals=0
        ),
        name=name,
    )(rows, right)


def fold_kernel(width, block, have_ref, *refs):
    received, (keep_ref, send_ref) = refs[:-2], refs[-2:]
    total = have_ref[:, :width]
    slot = have_ref[:, width:]
    for ref in received:
        total += ref[:, :width].astype(F32)
        slot += ref[:, width : width + LANES].astype(F32) + ref[:, width + LANES :].astype(F32)
    keep_ref[:, :width] = total[:block]
    keep_ref[:, width:] = slot[:block]
    send_ref[:, :width] = total[block:].astype(BF16)
    high, low = split_sum(slot[block:])
    send_ref[:, width : width + LANES] = high
    send_ref[:, width + LANES :] = low


def fold(have, received, block, width):
    return pl.pallas_call(
        functools.partial(fold_kernel, width, block),
        out_shape=(
            jax.ShapeDtypeStruct((block, width + LANES), F32),
            jax.ShapeDtypeStruct((have.shape[0] - block, width + 2 * LANES), BF16),
        ),
        in_specs=[VMEM] * (1 + len(received)),
        out_specs=(VMEM, VMEM),
        name="fold",
    )(have, *received)


def last_kernel(width, have_ref, *refs):
    received, (dx_ref, slot_ref) = refs[:-2], refs[-2:]
    total = have_ref[:, :width]
    slot = have_ref[:, width:]
    for ref in received:
        total += ref[:, :width].astype(F32)
        slot += ref[:, width : width + LANES].astype(F32) + ref[:, width + LANES :].astype(F32)
    dx_ref[...] = total
    slot_ref[...] = slot


def last(have, received, width):
    return pl.pallas_call(
        functools.partial(last_kernel, width),
        out_shape=(
            jax.ShapeDtypeStruct((have.shape[0], width), F32),
            jax.ShapeDtypeStruct((have.shape[0], LANES), F32),
        ),
        in_specs=[VMEM] * (1 + len(received)),
        out_specs=(VMEM, VMEM),
        name="last",
    )(have, *received)


def shift(value, axis, by):
    size = lax.axis_size(axis)
    return lax.ppermute(value, axis, [(i, (i + by) % size) for i in range(size)])


def spread(block, axis):
    size = lax.axis_size(axis)
    return jnp.concatenate([block] + [shift(block, axis, by) for by in range(1, size)], axis=0)


def collect(send, axis, block):
    size = lax.axis_size(axis)
    return [shift(send[(by - 1) * block : by * block], axis, -by) for by in range(1, size)]


def per_device(tokens, out_grad, expert_ids, probs, w_gate, w_up, w_down):
    count, width = tokens.shape
    owners = lax.axis_size("expert")
    expert = (lax.axis_index("expert") // (owners // EXPERTS)).astype(jnp.int32).reshape(1)
    lane = jnp.arange(LANES, dtype=jnp.int32)[None, :]
    extra = jnp.zeros((count, LANES), BF16)
    for k in range(TOP):
        hit = lane == expert_ids[:, k : k + 1] * TOP + k
        extra = jnp.where(hit, probs[:, k : k + 1], extra)
    rows = jnp.concatenate([tokens, out_grad, extra], axis=1)
    for axis in ("expert", "tensor", "seq"):
        rows = spread(rows, axis)
    block = rows.shape[0] // lax.axis_size("seq")
    keep, send, d_gate, d_up, grad_d = main_call(expert, rows, w_gate, w_up, w_down, block)
    received = collect(send, "seq", block)
    block //= lax.axis_size("tensor")
    keep, send = fold(keep, received, block, width)
    received = collect(send, "tensor", block)
    grad_g = outer_call(rows, d_gate, width, "outer_gate")
    block //= owners
    keep, send = fold(keep, received, block, width)
    received = collect(send, "expert", block)
    grad_u = outer_call(rows, d_up, width, "outer_up")
    grad_tokens, slot = last(keep, received, width)
    grad_probs = jnp.sum(slot[:, : EXPERTS * TOP].reshape(count, EXPERTS, TOP), axis=1)
    return (grad_tokens, grad_probs, grad_g, grad_u, grad_d)


def solution(mesh):
    placed = (
        P(("parts", "expert", "tensor", "seq"), None),
        P(("parts", "expert", "tensor", "seq"), None),
        P(("parts", "expert", "tensor", "seq"), None),
        P(("parts", "expert", "tensor", "seq"), None),
        P("expert", None, ("tensor", "seq")),
        P("expert", None, ("tensor", "seq")),
        P("expert", ("tensor", "seq"), None),
    )
    return jax.shard_map(
        per_device,
        mesh=mesh,
        in_specs=placed,
        out_specs=(
            P(("parts", "expert", "tensor", "seq"), None),
            P(("parts", "expert", "tensor", "seq"), None),
            P(("parts", "expert"), None, ("tensor", "seq")),
            P(("parts", "expert"), None, ("tensor", "seq")),
            P(("parts", "expert"), ("tensor", "seq"), None),
        ),
        check_vma=False,
    )
```
